32 devices in a mesh: grp: 2 (over x), dp: 4 (over y, core), mp: 4 (over z).
Axes of the slice: x: 2, y: 2, z: 4, core: 2. Of those that a mesh axis runs over, the one named last changes fastest.
Arguments:
- up_input: bfloat16 [8, 256, 4096], P(('grp', 'dp'), None, 'mp'), may hold values from -6 to 6
- gate_pre: bfloat16 [8, 256, 14336], P(('grp', 'dp'), None, 'mp'), may hold values from -6 to 6
- up_pre: bfloat16 [8, 256, 14336], P(('grp', 'dp'), None, 'mp'), may hold values from -6 to 6
- grad_hidden: bfloat16 [8, 256, 14336], P(('grp', 'dp'), None, 'mp'), may hold values from -6 to 6
- grad_output: bfloat16 [8, 256, 4096], P(('grp', 'dp'), None, 'mp'), may hold values from -6 to 6
- proj_up_in: bfloat16 [64, 4096], P(None, 'mp'), may hold values from -0.09375 to 0.09375
- proj_up_out: bfloat16 [64, 14336], P(None, 'mp'), may hold values from -0.046875 to 0.046875
- proj_down_in: bfloat16 [64, 14336], P(None, 'mp'), may hold values from -0.046875 to 0.046875
- proj_down_out: bfloat16 [64, 4096], P(None, 'mp'), may hold values from -0.09375 to 0.09375
- gram: float32 [8192, 8192], P(('grp', 'mp'), 'dp'), may hold values from -4 to 14
- canaries: bfloat16 [1024, 8192], P('dp', ('grp', 'mp')), may hold values from -6 to 6
Outputs:
- gram_new: float32 [8192, 8192], P(('grp', 'mp'), 'dp')
- mapped: bfloat16 [1024, 8192], P(('grp', 'mp'), 'dp')
- scores: float32 [8, 1024], P(None, ('grp', 'mp'))
The draws below stay inside these ranges and needn't reach their ends.
All inputs are finite; a program needn't handle non-finite values.
Results may differ from the reference program's by a relative error of at most 0.005.
Values may be sent and summed in bfloat16 or wider, within the bound.
No kernel may reach another device: no remote copies, remote signals or barrier semaphores. Data moves between devices by JAX's collectives and lax.ppermute only.
A program may use at most 64 MiB of HBM per device.

```python
import math
import jax
import jax.numpy as jnp
from jax import lax

D = 4096
FF = 14336
RANK = 64
SEQ = 256
CAN = 1024
SEQS = 8
ORDER = 8192


def draw_gram(key, part):
    first, second = jax.random.split(jax.random.fold_in(key, 17), 2)
    base = jnp.clip(jax.random.normal(first, (ORDER, ORDER), jnp.float32), -4.0, 4.0)
    symmetric = 0.5 * (base + base.T)
    diagonal = jnp.exp(jax.random.uniform(second, (ORDER,), jnp.float32, 0.0, math.log(10.0)))
    return symmetric + jnp.diag(diagonal)


def block_levels(stream_key, extent, shards, smallest, top_value):
    def one(axis_at, shards_of):
        steps = jax.random.uniform(jax.random.fold_in(jax.random.fold_in(stream_key, 6), axis_at), (shards_of,), jnp.float32, smallest / len(shards), top_value / len(shards))
        return jnp.repeat(jnp.exp(steps), extent[axis_at] // shards_of).reshape((-1,) + (1,) * (len(extent) - axis_at - 1))

    factor_of = one(*shards[0])
    for cut in shards[1:]:
        factor_of = factor_of * one(*cut)
    return factor_of


def scatter_about(own_key, dims, spread, limit, cuts=(), dtype=jnp.bfloat16):
    entries = spread * jax.random.normal(own_key, dims, jnp.float32)
    if cuts:
        entries = entries * block_levels(own_key, dims, cuts, -0.22, 0.18)
    return jnp.clip(entries, -limit, limit).astype(dtype)


def setup_inputs(seed: int = 0) -> dict:
    key_of = jax.random.split(jax.random.key(seed), 12)
    up_input = scatter_about(key_of[0], (SEQS, SEQ, D), 1.0, 6.0, ((0, 8), (2, 4)))
    gate_pre = scatter_about(key_of[1], (SEQS, SEQ, FF), 1.0, 6.0, ((0, 8), (2, 4)))
    up_pre = scatter_about(key_of[2], (SEQS, SEQ, FF), 1.0, 6.0, ((0, 8), (2, 4)))
    grad_hidden = scatter_about(key_of[3], (SEQS, SEQ, FF), 1.0, 6.0, ((0, 8), (2, 4)))
    grad_output = scatter_about(key_of[4], (SEQS, SEQ, D), 1.0, 6.0, ((0, 8), (2, 4)))
    proj_up_in = scatter_about(key_of[5], (RANK, D), D ** -0.5, 0.09375, ((1, 4),))
    proj_up_out = scatter_about(key_of[6], (RANK, FF), FF ** -0.5, 0.046875, ((1, 4),))
    proj_down_in = scatter_about(key_of[7], (RANK, FF), FF ** -0.5, 0.046875, ((1, 4),))
    proj_down_out = scatter_about(key_of[8], (RANK, D), D ** -0.5, 0.09375, ((1, 4),))
    gram = draw_gram(jax.random.fold_in(key_of[11], 71), 0)
    canaries = scatter_about(key_of[10], (CAN, ORDER), 1.0, 6.0, ((0, 4), (1, 8)))
    return {"up_input": up_input, "gate_pre": gate_pre, "up_pre": up_pre, "grad_hidden": grad_hidden, "grad_output": grad_output, "proj_up_in": proj_up_in, "proj_up_out": proj_up_out, "proj_down_in": proj_down_in, "proj_down_out": proj_down_out, "gram": gram, "canaries": canaries}


def project(values, matrix):
    return lax.dot_general(values, matrix, (((1,), (1,)), ((), ())), preferred_element_type=jnp.float32)

def sequence_row(pieces, proj_up_in, proj_up_out, proj_down_in, proj_down_out):
    up_input, gate_pre, up_pre, grad_hidden, grad_output = pieces
    gate_act = jax.nn.silu(gate_pre.astype(jnp.float32))
    grad_up = (grad_hidden.astype(jnp.float32) * gate_act).astype(jnp.bfloat16)
    hidden = (gate_act * up_pre.astype(jnp.float32)).astype(jnp.bfloat16)
    in_up = project(up_input, proj_up_in)
    out_up = project(grad_up, proj_up_out)
    in_down = project(hidden, proj_down_in)
    out_down = project(grad_output, proj_down_out)
    norm_len = 1.0 / math.sqrt(SEQ)
    up_feat = jnp.dot(out_up.T, in_up, precision=lax.Precision.HIGHEST) * norm_len
    down_feat = jnp.dot(out_down.T, in_down, precision=lax.Precision.HIGHEST) * norm_len
    return jnp.concatenate([up_feat.reshape(-1), down_feat.reshape(-1)])

def reference(up_input, gate_pre, up_pre, grad_hidden, grad_output, proj_up_in, proj_up_out, proj_down_in, proj_down_out, gram, canaries):

    def one_row(pieces):
        return sequence_row(pieces, proj_up_in, proj_up_out, proj_down_in, proj_down_out)
    features = lax.map(one_row, (up_input, gate_pre, up_pre, grad_hidden, grad_output))
    gram_new = gram + jnp.dot(features.T, features, precision=lax.Precision.HIGHEST) / SEQS
    gram_low = gram_new.astype(jnp.bfloat16)
    norm_order = 1.0 / math.sqrt(ORDER)
    mapped_full = jnp.dot(canaries, gram_low, preferred_element_type=jnp.float32) * norm_order
    scores = jnp.dot(features, mapped_full.T, precision=lax.Precision.HIGHEST) * norm_order
    return (gram_new, mapped_full.astype(jnp.bfloat16), scores)
```

```python
import functools
import math

import jax
import jax.numpy as jnp
from jax import lax
from jax.experimental import pallas as pl
from jax.experimental.pallas import tpu as pltpu
from jax.sharding import PartitionSpec as P

LANES = 128
NT = (((1,), (1,)), ((), ()))
TN = (((0,), (0,)), ((), ()))
VMEM_LIMIT = 48 * 1024 * 1024


def dot(a, b, dims, precision=None):
    return lax.dot_general(a, b, dims, precision=precision, preferred_element_type=jnp.float32)


def pairs(size, bit):
    return [(at, at ^ bit) for at in range(size)]


def bits_of(size):
    return [1 << at for at in reversed(range(size.bit_length() - 1))]


def params():
    return pltpu.CompilerParams(vmem_limit_bytes=VMEM_LIMIT)


def cost(flops, bytes_accessed):
    return pl.CostEstimate(flops=flops, bytes_accessed=bytes_accessed, transcendentals=0)


def project_kernel(mp, me, up_in, gate, up_pre, grad_h, grad_o, p_ui, p_uo, p_di, p_do, *rest):
    outs, (whole, out_up, in_down) = rest[:mp], rest[mp:]
    step = pl.program_id(0)
    act = gate[...].astype(jnp.float32)
    act = act / (1.0 + jnp.exp(-act))
    grad_up = (grad_h[...].astype(jnp.float32) * act).astype(jnp.bfloat16)
    hidden = (act * up_pre[...].astype(jnp.float32)).astype(jnp.bfloat16)
    part_up = dot(grad_up, p_uo[...], NT)
    part_down = dot(hidden, p_di[...], NT)

    @pl.when(step == 0)
    def _():
        out_up[...] = part_up
        in_down[...] = part_down

    @pl.when(step > 0)
    def _():
        out_up[...] += part_up
        in_down[...] += part_down

    @pl.when(step == pl.num_programs(0) - 1)
    def _():
        in_up = dot(up_in[...], p_ui[...], NT)
        out_down = dot(grad_o[...], p_do[...], NT)
        whole[...] = jnp.concatenate([in_up, out_up[...], in_down[...], out_down], axis=1)
        rows = outs[0].shape[0]
        own = me[0] % mp
        for at, out in enumerate(outs):
            out[...] = whole[pl.ds(pl.multiple_of((own ^ at) * rows, rows), rows), :]


def project_all(mp, me, up_in, gate, up_pre, grad_h, grad_o, p_ui, p_uo, p_di, p_do):
    _, seq, d_here = up_in.shape
    f_here = gate.shape[2]
    rank = p_ui.shape[0]
    tile = max(t for t in range(LANES, 897, LANES) if f_here % t == 0)
    wide = pl.BlockSpec((None, seq, tile), lambda i, me: (0, 0, i))
    narrow = pl.BlockSpec((None, seq, d_here), lambda i, me: (0, 0, 0))
    wide_p = pl.BlockSpec((rank, tile), lambda i, me: (0, i))
    narrow_p = pl.BlockSpec((rank, d_here), lambda i, me: (0, 0))
    rows = seq // mp
    return pl.pallas_call(
        functools.partial(project_kernel, mp),
        out_shape=[jax.ShapeDtypeStruct((rows, 4 * rank), jnp.float32)] * mp,
        grid_spec=pltpu.PrefetchScalarGridSpec(
            num_scalar_prefetch=1,
            grid=(f_here // tile,),
            in_specs=[narrow, wide, wide, wide, narrow, narrow_p, wide_p, wide_p, narrow_p],
            out_specs=[pl.BlockSpec((rows, 4 * rank), lambda i, me: (0, 0))] * mp,
            scratch_shapes=[
                pltpu.VMEM((seq, 4 * rank), jnp.float32),
                pltpu.VMEM((seq, rank), jnp.float32),
                pltpu.VMEM((seq, rank), jnp.float32),
            ],
        ),
        compiler_params=params(),
        cost_estimate=cost(4 * seq * rank * (d_here + f_here), 6 * seq * f_here + 4 * seq * d_here),
    )(me, up_in, gate, up_pre, grad_h, grad_o, p_ui, p_uo, p_di, p_do)


def feature_kernel(norm, rank, *refs):
    parts, out, (square,) = refs[:-2], refs[-2], refs[-1:]
    total = parts[0][...]
    for part in parts[1:]:
        total = total + part[...]
    half = rank * rank // LANES
    for at in range(2):
        left = total[:, (2 * at + 1) * rank : (2 * at + 2) * rank]
        right = total[:, 2 * at * rank : (2 * at + 1) * rank]
        square[...] = dot(left, right, TN, lax.Precision.HIGHEST) * norm
        step = LANES // rank
        out[at * half : (at + 1) * half, :] = jnp.concatenate(
            [square[pl.ds(lane, half, step), :] for lane in range(step)], axis=1
        )


def feature_rows(norm, rank, parts):
    return pl.pallas_call(
        functools.partial(feature_kernel, norm, rank),
        out_shape=jax.ShapeDtypeStruct((2 * rank * rank // LANES, LANES), jnp.float32),
        scratch_shapes=[pltpu.VMEM((rank, rank), jnp.float32)],
        compiler_params=params(),
        cost_estimate=cost(24 * rank * rank * parts[0].shape[0], 100000),
    )(*parts)


def spread_kernel(seqs, dp, mp, me, gathered, left, right, thin, col, rows_f, cols_f):
    grp_at, dp_at, mp_at = me[0] // (dp * mp), (me[0] // mp) % dp, me[0] % mp
    own = grp_at * dp + dp_at
    row_at = grp_at * mp + mp_at
    count = seqs.bit_length() - 1
    row_groups, col_groups = rows_f.shape[1] // LANES, cols_f.shape[1] // LANES
    for seq in range(seqs):
        code = own ^ seq
        place = 0
        for bit in range(count):
            place = place + (((code >> bit) & 1) << (count - 1 - bit))
        for group in range(row_groups):
            rows_f[seq : seq + 1, group * LANES : (group + 1) * LANES] = gathered[
                place, pl.ds(row_at * row_groups + group, 1), :
            ]
        for group in range(col_groups):
            cols_f[seq : seq + 1, group * LANES : (group + 1) * LANES] = gathered[
                place, pl.ds(dp_at * col_groups + group, 1), :
            ]
    row, column = rows_f[...], cols_f[...]
    row_high = row.astype(jnp.bfloat16).astype(jnp.float32)
    col_high = column.astype(jnp.bfloat16).astype(jnp.float32)
    row_low, col_low = row - row_high, column - col_high
    for out, stack in (
        (left, [row_high, row_high, row_low]),
        (right, [col_high, col_low, col_high]),
        (thin, [row_high, row_low]),
    ):
        spare = out.shape[0] - len(stack) * seqs
        if spare:
            stack.append(jnp.zeros((spare, out.shape[1]), jnp.float32))
        out[...] = jnp.concatenate(stack).astype(jnp.bfloat16)
    col[...] = column


def spread(me, gathered, dp, mp, rows_here, cols_here):
    seqs = gathered.shape[0]
    deep = -(-3 * seqs // 16) * 16
    thin = -(-2 * seqs // LANES) * LANES
    return pl.pallas_call(
        functools.partial(spread_kernel, seqs, dp, mp),
        out_shape=[
            jax.ShapeDtypeStruct((deep, rows_here), jnp.bfloat16),
            jax.ShapeDtypeStruct((deep, cols_here), jnp.bfloat16),
            jax.ShapeDtypeStruct((thin, rows_here), jnp.bfloat16),
            jax.ShapeDtypeStruct((seqs, cols_here), jnp.float32),
        ],
        in_specs=[
            pl.BlockSpec(memory_space=pltpu.SMEM),
            pl.BlockSpec(memory_space=pltpu.VMEM),
        ],
        scratch_shapes=[
            pltpu.VMEM((seqs, rows_here), jnp.float32),
            pltpu.VMEM((seqs, cols_here), jnp.float32),
        ],
        compiler_params=params(),
        cost_estimate=cost(0, 1000000),
    )(me, gathered)


def update_kernel(scale, gram, left, right, out):
    out[...] = gram[...] + dot(left[...], right[...], TN) * scale


def update(scale, gram, left, right):
    rows, cols = gram.shape
    tile = min(rows, 128)
    deep = left.shape[0]
    return pl.pallas_call(
        functools.partial(update_kernel, scale),
        out_shape=jax.ShapeDtypeStruct(gram.shape, jnp.float32),
        grid=(rows // tile,),
        in_specs=[
            pl.BlockSpec((tile, cols), lambda i: (i, 0)),
            pl.BlockSpec((deep, tile), lambda i: (0, i)),
            pl.BlockSpec((deep, cols), lambda i: (0, 0)),
        ],
        out_specs=pl.BlockSpec((tile, cols), lambda i: (i, 0)),
        compiler_params=params(),
        cost_estimate=cost(2 * rows * cols * deep, 8 * rows * cols),
    )(gram, left, right)


def product_kernel(n_low, has_more, has_recv, me, can, gram, *rest):
    rest = list(rest)
    more = rest.pop(0) if has_more else None
    recv = rest.pop(0) if has_recv else None
    low = rest.pop(0)
    keep = rest.pop(0) if rest[1:] else None
    gram_low = rest.pop(0)
    step = pl.program_id(0)
    width = gram.shape[1]

    @pl.when(step == 0)
    def _():
        gram_low[...] = gram[...].astype(jnp.bfloat16)

    rows = can[...].reshape(-1, can.shape[-1])
    value = dot(rows, gram_low[...], (((1,), (0,)), ((), ())))
    if has_more:
        value = jnp.concatenate([value, dot(rows, more[...], NT)], axis=1)
    if has_recv:
        value = value + recv[...].astype(jnp.float32)
    if keep is None:
        low[...] = value.astype(jnp.bfloat16)
    else:

        @pl.when(step < n_low)
        def _():
            low[...] = value.astype(jnp.bfloat16)

        @pl.when(step >= n_low)
        def _():
            keep[...] = value


def product(where, me, can, gram, more, recv, piece, width, first, count, n_low, chunk):
    units, unit, depth = can.shape
    per = chunk // unit
    full = width + (more.shape[0] if more is not None else 0)
    in_specs = [
        pl.BlockSpec((per, unit, depth), lambda i, me: (where(me[0], first + i), 0, 0)),
        pl.BlockSpec((depth, width), lambda i, me: (0, piece)),
    ]
    args = [can, gram]
    if more is not None:
        in_specs.append(pl.BlockSpec(more.shape, lambda i, me: (0, 0)))
        args.append(more)
    if recv is not None:
        in_specs.append(pl.BlockSpec((chunk, full), lambda i, me: (i, 0)))
        args.append(recv)
    out_shape = [jax.ShapeDtypeStruct((n_low * chunk, full), jnp.bfloat16)]
    out_specs = [pl.BlockSpec((chunk, full), lambda i, me: (jnp.minimum(i, n_low - 1), 0))]
    if count > n_low:
        out_shape.append(jax.ShapeDtypeStruct(((count - n_low) * chunk, full), jnp.float32))
        out_specs.append(
            pl.BlockSpec((chunk, full), lambda i, me: (jnp.maximum(i - n_low, 0), 0))
        )
    return pl.pallas_call(
        functools.partial(product_kernel, n_low, more is not None, recv is not None),
        out_shape=out_shape,
        grid_spec=pltpu.PrefetchScalarGridSpec(
            num_scalar_prefetch=1,
            grid=(count,),
            in_specs=in_specs,
            out_specs=out_specs,
            scratch_shapes=[pltpu.VMEM((depth, width), jnp.bfloat16)],
        ),
        compiler_params=params(),
        cost_estimate=cost(2 * count * chunk * full * depth, 4 * depth * width + 2 * count * chunk * (depth + full)),
    )(me, *args)


def finish_kernel(seqs, scale, norm, pieces, *refs):
    own, (col, mapped, scores) = refs[:-3], refs[-3:]
    column = col[...]
    values = []
    for at in range(len(own) // pieces):
        terms = own[at * pieces : (at + 1) * pieces]
        value = terms[0][...]
        for term in terms[1:]:
            value = value + term[...].astype(jnp.float32)
        values.append(value)
    width = values[0].shape[1]
    last = values[-1]
    thin = last[:, width:]
    thin = (thin[:, :seqs] + thin[:, seqs : 2 * seqs]) * scale
    values[-1] = last[:, :width]
    whole = jnp.concatenate(values, axis=1)
    whole = whole + dot(thin, column, (((1,), (0,)), ((), ())), lax.Precision.HIGHEST)
    whole = whole * norm
    mapped[...] = whole.astype(jnp.bfloat16)
    scores[...] = dot(column, whole, NT, lax.Precision.HIGHEST) * norm


def finish(scale, norm, kept, col, chunk):
    seqs, cols = col.shape
    in_specs, args = [], []
    for keep, arrived in kept:
        in_specs.append(pl.BlockSpec((chunk, keep.shape[1]), lambda i, n=keep.shape[0]: (n // chunk - 1, 0)))
        args.append(keep)
        for array in arrived:
            in_specs.append(pl.BlockSpec((chunk, array.shape[1]), lambda i, n=array.shape[0]: (n // chunk - 1, 0)))
            args.append(array)
    in_specs.append(pl.BlockSpec((seqs, cols), lambda i: (0, 0)))
    return pl.pallas_call(
        functools.partial(finish_kernel, seqs, scale, norm, len(args) // len(kept)),
        out_shape=[
            jax.ShapeDtypeStruct((chunk, cols), jnp.bfloat16),
            jax.ShapeDtypeStruct((seqs, chunk), jnp.float32),
        ],
        grid=(1,),
        in_specs=in_specs,
        out_specs=[
            pl.BlockSpec((chunk, cols), lambda i: (0, 0)),
            pl.BlockSpec((seqs, chunk), lambda i: (0, 0)),
        ],
        compiler_params=params(),
        cost_estimate=cost(24 * chunk * cols * seqs, 14 * chunk * cols),
    )(*args, col)


def shards(
    sizes,
    up_input,
    gate_pre,
    up_pre,
    grad_hidden,
    grad_output,
    proj_up_in,
    proj_up_out,
    proj_down_in,
    proj_down_out,
    gram,
    canaries,
):
    grp, dp, mp = sizes
    rank = proj_up_in.shape[0]
    seq_len = up_input.shape[1]
    rows_here, cols_here = gram.shape
    features = rows_here * grp * mp
    can_here = canaries.shape[0]
    chunk = can_here * dp // (grp * mp)
    me = lax.axis_index(("grp", "dp", "mp")).astype(jnp.int32).reshape(1)

    direct = can_here >= chunk
    if direct:
        blocks = {0: canaries}
        for bit in bits_of(dp):
            blocks |= {at ^ bit: lax.ppermute(block, "dp", pairs(dp, bit)) for at, block in blocks.items()}
        can = jnp.concatenate([blocks[at] for at in range(dp)])
    else:
        can = lax.all_gather(canaries, "dp", axis=0, tiled=True)
    can = can.reshape(-1, chunk, canaries.shape[1])

    codes = [0]
    halvings = [("grp", grp, bit, bit * mp) for bit in bits_of(grp)]
    halvings += [("mp", mp, bit, bit) for bit in reversed(bits_of(mp))]
    for _, _, _, code in reversed(halvings):
        codes = [at | code for at in codes] + codes

    def where(me, at):
        code = 0
        for place, value in enumerate(codes):
            code = jnp.where(at == place, value, code) if place else jnp.int32(value)
        target = ((me // (dp * mp)) * mp + me % mp) ^ code
        if not direct:
            return target
        row = target * chunk
        block = (row // can_here) ^ ((me // mp) % dp)
        return (block * can_here + row % can_here) // chunk

    parts = project_all(
        mp, me, up_input, gate_pre, up_pre, grad_hidden, grad_output,
        proj_up_in, proj_up_out, proj_down_in, proj_down_out,
    )
    parts = [parts[0]] + [lax.ppermute(parts[at], "mp", pairs(mp, at)) for at in range(1, mp)]
    row = feature_rows(1.0 / math.sqrt(seq_len), rank, parts)
    for bit in reversed(bits_of(mp)):
        row = row + lax.ppermute(row, "mp", pairs(mp, bit))
    gathered = row[None]
    for axis, size in (("grp", grp), ("dp", dp)):
        for bit in bits_of(size):
            gathered = jnp.concatenate([gathered, lax.ppermute(gathered, axis, pairs(size, bit))])
    left, right, thin, col = spread(me, gathered, dp, mp, rows_here, cols_here)
    seqs = gathered.shape[0]
    gram_new = update(1.0 / seqs, gram, left, right)

    width = max(LANES, cols_here // 4)
    n_pieces = cols_here // width
    total = grp * mp
    kept = []
    for piece in range(n_pieces):
        more = thin if piece == n_pieces - 1 else None
        take = functools.partial(product, where, me, can, gram, more)
        axis, size, bit, _ = halvings[0]
        (low,) = take(None, piece, width, 0, total // 2, total // 2, chunk)
        recv = lax.ppermute(low, axis, pairs(size, bit))
        left_over = total // 2
        low, keep = take(recv, piece, width, total // 2, left_over, left_over // 2, chunk)
        arrived = []
        for at, (axis, size, bit, _) in enumerate(halvings[1:]):
            recv = lax.ppermute(low, axis, pairs(size, bit))
            arrived.append(recv)
            left_over //= 2
            if left_over > 1:
                half = (left_over // 2) * chunk
                low = keep[:half]
                for array in arrived:
                    low = low + array[-left_over * chunk :][:half].astype(jnp.float32)
                low = low.astype(jnp.bfloat16)
                keep = keep[half:]
        kept.append((keep, arrived))
    norm = 1.0 / math.sqrt(features)
    mapped, scores = finish(1.0 / seqs, norm, kept, col, chunk)
    for bit in bits_of(dp):
        scores = scores + lax.ppermute(scores, "dp", pairs(dp, bit))
    return gram_new, mapped, scores


def solution(mesh):
    sizes = tuple(mesh.shape[name] for name in ("grp", "dp", "mp"))
    wide = P(("grp", "dp"), None, "mp")
    return jax.shard_map(
        functools.partial(shards, sizes),
        mesh=mesh,
        in_specs=(wide, wide, wide, wide, wide)
        + (P(None, "mp"),) * 4
        + (P(("grp", "mp"), "dp"), P("dp", ("grp", "mp"))),
        out_specs=(P(("grp", "mp"), "dp"), P(("grp", "mp"), "dp"), P(None, ("grp", "mp"))),
        check_vma=False,
    )
```

```python
import functools
import math

import jax
import jax.numpy as jnp
from jax import lax
from jax.experimental import pallas as pl
from jax.experimental.pallas import tpu as pltpu
from jax.sharding import PartitionSpec as P

LANES = 128
NT = (((1,), (1,)), ((), ()))
TN = (((0,), (0,)), ((), ()))
VMEM_LIMIT = 24 * 1024 * 1024


def dot(a, b, dims, precision=None):
    return lax.dot_general(a, b, dims, precision=precision, preferred_element_type=jnp.float32)


def pairs(size, bit):
    return [(at, at ^ bit) for at in range(size)]


def bits_of(size):
    return [1 << at for at in reversed(range(size.bit_length() - 1))]


def params():
    return pltpu.CompilerParams(vmem_limit_bytes=VMEM_LIMIT)


def cost(flops, bytes_accessed):
    return pl.CostEstimate(flops=flops // 100, bytes_accessed=bytes_accessed // 100, transcendentals=0)


def project_kernel(order, tile, me, *refs):
    sources, (sent, kept, gram, gram_low), (held, whole, arrived) = refs[:10], refs[10:14], (refs[14:23], refs[23], refs[24])
    copies = {}

    def copy(name, source, target):
        one = pltpu.make_async_copy(source, target, arrived.at[len(copies)])
        one.start()
        copies[name] = one

    up_in, gate, up_pre, grad_h, grad_o, p_ui, p_uo, p_di, p_do, old = sources
    h_up_in, h_gate, h_up_pre, h_grad_h, h_grad_o, h_ui, h_uo, h_di, h_do = held
    starts = range(0, h_gate.shape[1], tile)
    for start in starts:
        part = pl.ds(start, tile)
        for name, source, target in (("gate", gate, h_gate), ("grad_h", grad_h, h_grad_h), ("up_pre", up_pre, h_up_pre)):
            copy((name, start), source.at[0, :, part], target.at[:, part])
        for name, source, target in (("uo", p_uo, h_uo), ("di", p_di, h_di)):
            copy((name, start), source.at[:, part], target.at[:, part])
    copy("up_in", up_in.at[0], h_up_in)
    copy("ui", p_ui, h_ui)
    copy("grad_o", grad_o.at[0], h_grad_o)
    copy("do", p_do, h_do)
    share = gram.shape[0] // 4
    for at in range(4):
        rows = pl.ds(at * share, share)
        copy(("gram", at), old.at[rows], gram.at[rows])

    out_up, in_down = 0.0, 0.0
    for start in starts:
        part = slice(start, start + tile)
        for name in ("gate", "grad_h", "up_pre", "uo", "di"):
            copies[name, start].wait()
        act = h_gate[:, part].astype(jnp.float32)
        act = act / (1.0 + jnp.exp(-act))
        grad_up = (h_grad_h[:, part].astype(jnp.float32) * act).astype(jnp.bfloat16)
        hidden = (act * h_up_pre[:, part].astype(jnp.float32)).astype(jnp.bfloat16)
        out_up = out_up + dot(grad_up, h_uo[:, part], NT)
        in_down = in_down + dot(hidden, h_di[:, part], NT)
    for name in ("up_in", "ui", "grad_o", "do"):
        copies[name].wait()
    in_up = dot(h_up_in[...], h_ui[...], NT)
    out_down = dot(h_grad_o[...], h_do[...], NT)
    whole[...] = jnp.concatenate([in_up, out_up, in_down, out_down], axis=1)
    rows = whole.shape[0] // len(order)
    own = me[0] % len(order)
    for at, code in enumerate(order):
        out = sent if at < len(order) // 2 else kept
        spot = at % (len(order) // 2) * rows
        out[spot : spot + rows, :] = whole[pl.ds(pl.multiple_of((own ^ code) * rows, rows), rows), :]
    for at in range(4):
        copies["gram", at].wait()
        rows = slice(at * share, (at + 1) * share)
        gram_low[rows, :] = gram[rows, :].astype(jnp.bfloat16)


def project_all(order, me, up_in, gate, up_pre, grad_h, grad_o, p_ui, p_uo, p_di, p_do, gram):
    _, seq, d_here = up_in.shape
    f_here = gate.shape[2]
    rank = p_ui.shape[0]
    tile = max(t for t in range(LANES, 897, LANES) if f_here % t == 0)
    arrays = (up_in, gate, up_pre, grad_h, grad_o, p_ui, p_uo, p_di, p_do)
    vmem = pl.BlockSpec(memory_space=pltpu.VMEM)
    return pl.pallas_call(
        functools.partial(project_kernel, order, tile),
        out_shape=[jax.ShapeDtypeStruct((seq // 2, 4 * rank), jnp.float32)] * 2
        + [jax.ShapeDtypeStruct(gram.shape, dtype) for dtype in (jnp.float32, jnp.bfloat16)],
        in_specs=[pl.BlockSpec(memory_space=pltpu.SMEM)] + [pl.BlockSpec(memory_space=pltpu.HBM)] * 10,
        out_specs=[vmem] * 4,
        scratch_shapes=[pltpu.VMEM(array.shape[-2:], array.dtype) for array in arrays]
        + [
            pltpu.VMEM((seq, 4 * rank), jnp.float32),
            pltpu.SemaphoreType.DMA((5 * (f_here // tile) + 8,)),
        ],
        compiler_params=params(),
        cost_estimate=cost(4 * seq * rank * (d_here + f_here), 6 * seq * f_here + 4 * seq * d_here),
    )(me, *(pltpu.with_memory_space_constraint(array, pltpu.HBM) for array in (*arrays, gram)))


def feature_kernel(norm, rank, mine, there, out, square):
    rows = there.shape[0]
    total = mine[mine.shape[0] - rows :, :] + there[...]
    half = rank * rank // LANES
    for at in range(2):
        left = total[:, (2 * at + 1) * rank : (2 * at + 2) * rank]
        right = total[:, 2 * at * rank : (2 * at + 1) * rank]
        square[...] = dot(left, right, TN, lax.Precision.HIGHEST) * norm
        step = LANES // rank
        out[at * half : (at + 1) * half, :] = jnp.concatenate(
            [square[pl.ds(lane, half, step), :] for lane in range(step)], axis=1
        )


def feature_rows(norm, rank, mine, there):
    return pl.pallas_call(
        functools.partial(feature_kernel, norm, rank),
        out_shape=jax.ShapeDtypeStruct((2 * rank * rank // LANES, LANES), jnp.float32),
        scratch_shapes=[pltpu.VMEM((rank, rank), jnp.float32)],
        compiler_params=params(),
        cost_estimate=cost(24 * rank * rank * there.shape[0], 100000),
    )(mine, there)


def spread_kernel(seqs, dp, mp, me, gathered, left, right, col, rows_f, cols_f):
    grp_at, dp_at, mp_at = me[0] // (dp * mp), (me[0] // mp) % dp, me[0] % mp
    own = grp_at * dp + dp_at
    row_at = grp_at * mp + mp_at
    count = seqs.bit_length() - 1
    row_groups, col_groups = rows_f.shape[1] // LANES, cols_f.shape[1] // LANES
    for seq in range(seqs):
        code = own ^ seq
        place = 0
        for bit in range(count):
            place = place + (((code >> bit) & 1) << (count - 1 - bit))
        for group in range(row_groups):
            rows_f[seq : seq + 1, group * LANES : (group + 1) * LANES] = gathered[
                place, pl.ds(row_at * row_groups + group, 1), :
            ]
        for group in range(col_groups):
            cols_f[seq : seq + 1, group * LANES : (group + 1) * LANES] = gathered[
                place, pl.ds(dp_at * col_groups + group, 1), :
            ]
    row, column = rows_f[...], cols_f[...]
    row_high = row.astype(jnp.bfloat16).astype(jnp.float32)
    col_high = column.astype(jnp.bfloat16).astype(jnp.float32)
    row_low, col_low = row - row_high, column - col_high
    for out, stack in (
        (left, [row_high, row_high, row_low]),
        (right, [col_high, col_low, col_high]),
    ):
        spare = out.shape[0] - len(stack) * seqs
        if spare:
            stack.append(jnp.zeros((spare, out.shape[1]), jnp.float32))
        out[...] = jnp.concatenate(stack).astype(jnp.bfloat16)
    col[...] = column


def spread(me, gathered, dp, mp, rows_here, cols_here):
    seqs = gathered.shape[0]
    deep = -(-3 * seqs // 16) * 16
    return pl.pallas_call(
        functools.partial(spread_kernel, seqs, dp, mp),
        out_shape=[
            jax.ShapeDtypeStruct((deep, rows_here), jnp.bfloat16),
            jax.ShapeDtypeStruct((deep, cols_here), jnp.bfloat16),
            jax.ShapeDtypeStruct((seqs, cols_here), jnp.float32),
        ],
        in_specs=[
            pl.BlockSpec(memory_space=pltpu.SMEM),
            pl.BlockSpec(memory_space=pltpu.VMEM),
        ],
        scratch_shapes=[
            pltpu.VMEM((seqs, rows_here), jnp.float32),
            pltpu.VMEM((seqs, cols_here), jnp.float32),
        ],
        compiler_params=params(),
        cost_estimate=cost(0, 1000000),
    )(me, gathered)


def update_kernel(scale, me, gram, left, right, out):
    rows = out.shape[0]
    at = pl.ds(pl.multiple_of(pl.program_id(0) * rows, rows), rows)
    out[...] = gram[at, :] + dot(left[...], right[...], TN) * scale


def update(scale, me, gram, left, right):
    rows, cols = gram.shape
    tile = min(rows, 256)
    deep = left.shape[0]
    return pl.pallas_call(
        functools.partial(update_kernel, scale),
        out_shape=jax.ShapeDtypeStruct(gram.shape, jnp.float32),
        grid=(rows // tile,),
        in_specs=[
            pl.BlockSpec(memory_space=pltpu.SMEM),
            pl.BlockSpec(memory_space=pltpu.VMEM),
            pl.BlockSpec((deep, tile), lambda i: (0, i)),
            pl.BlockSpec((deep, cols), lambda i: (0, 0)),
        ],
        out_specs=pl.BlockSpec((tile, cols), lambda i: (i, 0)),
        compiler_params=params(),
        cost_estimate=cost(2 * rows * cols * deep, 8 * rows * cols),
    )(me, gram, left, right)


def place(me, sizes, direct, bits, at, row, per):
    grp, dp, mp = sizes
    target = ((at ^ ((me // mp) % dp)) * per + row) if direct else row
    code = target ^ ((me // (dp * mp)) * mp + me % mp)
    spot = 0
    for bit in bits:
        spot = 2 * spot + (1 - ((code // bit) & 1))
    return spot


def sort_rows(me, sizes, direct, bits, first, count, cans, out):
    for at, can in enumerate(cans):
        for row in range(can.shape[0]):
            spot = place(me, sizes, direct, bits, at, row, can.shape[0]) - first

            @pl.when((spot >= 0) & (spot < count))
            def _(can=can, row=row, spot=spot):
                out[spot] = can[row]


def product_kernel(sizes, direct, bits, first, start, n_cans, n_recv, me, *refs):
    cans, gram, recvs, outs = refs[:n_cans], refs[n_cans], refs[n_cans + 1 : n_cans + 1 + n_recv], refs[n_cans + 1 + n_recv :]
    outs, rows = outs[:-1], outs[-1]
    low = outs[0]
    count, unit, depth = rows.shape
    sort_rows(me[0], sizes, direct, bits, first, count, cans, rows)
    width = low.shape[1]
    tile = min(width, 512)
    for at in range(0, width, tile):
        value = dot(
            rows[...].reshape(count * unit, depth),
            gram[:, start + at : start + at + tile],
            (((1,), (0,)), ((), ())),
        )
        if not recvs:
            low[:, at : at + tile] = value.astype(jnp.bfloat16)
        else:
            value = value + recvs[0][:, at : at + tile].astype(jnp.float32)
            half = low.shape[0]
            low[:, at : at + tile] = value[:half].astype(jnp.bfloat16)
            outs[1][:, at : at + tile] = value[half:]


def product(sizes, direct, bits, me, cans, gram, recvs, start, width):
    depth = gram.shape[0]
    unit = cans[0].shape[1]
    count = sizes[0] * sizes[2] // 2
    rows = count * unit
    vmem = pl.BlockSpec(memory_space=pltpu.VMEM)
    args = [me, *cans, gram, *recvs]
    if recvs:
        out_shape = [
            jax.ShapeDtypeStruct((rows // 2, width), jnp.bfloat16),
            jax.ShapeDtypeStruct((rows // 2, width), jnp.float32),
        ]
    else:
        out_shape = [jax.ShapeDtypeStruct((rows, width), jnp.bfloat16)]
    first = count if recvs else 0
    return pl.pallas_call(
        functools.partial(product_kernel, sizes, direct, bits, first, start, len(cans), len(recvs)),
        out_shape=out_shape,
        in_specs=[pl.BlockSpec(memory_space=pltpu.SMEM)] + [vmem] * (len(args) - 1),
        out_specs=[vmem] * len(out_shape),
        scratch_shapes=[pltpu.VMEM((count, unit, depth), jnp.bfloat16)],
        compiler_params=params(),
        cost_estimate=cost(2 * rows * width * depth, 2 * depth * width + 2 * rows * (depth + width)),
    )(*args)


def thin_kernel(sizes, direct, bits, n_cans, seqs, me, *refs):
    halves = refs[:n_cans], refs[n_cans : 2 * n_cans]
    gram, row, col, out, rows = refs[2 * n_cans :]
    count, _, unit, depth = rows.shape
    for half, cans in enumerate(halves):
        for at, can in enumerate(cans):
            for spot in range(can.shape[0]):
                rows[place(me[0], sizes, direct, bits, at, spot, can.shape[0]), half] = can[spot]

    def stack(*values):
        split = []
        for value in values:
            high = value.astype(jnp.bfloat16).astype(jnp.float32)
            split += [high, value - high]
        spare = -len(split) * seqs % LANES
        if spare:
            split.append(jnp.zeros((spare, values[0].shape[1]), jnp.float32))
        return jnp.concatenate(split).astype(jnp.bfloat16)

    across = dot(gram[...], stack(col[...]), NT).T
    across = across[:seqs] + across[seqs : 2 * seqs]
    own = row[:seqs].astype(jnp.float32) + row[2 * seqs : 3 * seqs].astype(jnp.float32)
    value = dot(rows[...].reshape(-1, depth), stack(own, across), NT).T
    out[:seqs] = value[:seqs] + value[seqs : 2 * seqs]
    out[seqs:] = value[2 * seqs : 3 * seqs] + value[3 * seqs : 4 * seqs]


def thin_products(sizes, direct, bits, me, halves, gram, left, col):
    seqs = col.shape[0]
    count = sizes[0] * sizes[2]
    unit, depth = halves[0][0].shape[1:]
    rows = count * 2 * unit
    vmem = pl.BlockSpec(memory_space=pltpu.VMEM)
    args = [*halves[0], *halves[1], gram, left, col]
    return pl.pallas_call(
        functools.partial(thin_kernel, sizes, direct, bits, len(halves[0]), seqs),
        out_shape=jax.ShapeDtypeStruct((2 * seqs, rows), jnp.float32),
        in_specs=[pl.BlockSpec(memory_space=pltpu.SMEM)] + [vmem] * len(args),
        out_specs=vmem,
        scratch_shapes=[pltpu.VMEM((count, 2, unit, depth), jnp.bfloat16)],
        compiler_params=params(),
        cost_estimate=cost(256 * depth * (gram.shape[1] + rows), 2 * depth * (gram.shape[1] + rows)),
    )(me, *args)


def score_kernel(scale, norm, thin, col, out):
    column = col[...]
    seqs = column.shape[0]
    inner = dot(column, column, NT, lax.Precision.HIGHEST) * scale
    value = thin[seqs:] + dot(inner, thin[:seqs], (((1,), (0,)), ((), ())), lax.Precision.HIGHEST)
    out[...] = value * norm


def score(scale, norm, thin, col):
    return pl.pallas_call(
        functools.partial(score_kernel, scale, norm),
        out_shape=jax.ShapeDtypeStruct((col.shape[0], thin.shape[1]), jnp.float32),
        compiler_params=params(),
        cost_estimate=cost(12 * col.size * col.shape[0], 8 * col.size),
    )(thin, col)


def finish_kernel(seqs, scale, norm, spots, *refs):
    terms, (thin, col, mapped) = list(refs[:-3]), refs[-3:]
    for number, row, column, rows, width in spots:
        value = 0.0
        for _ in range(number):
            term = terms.pop(0)
            value = value + term[term.shape[0] - rows :, :].astype(jnp.float32)
        share = dot(thin[:seqs, row : row + rows], col[:, column : column + width], TN, lax.Precision.HIGHEST)
        mapped[row : row + rows, column : column + width] = ((value + share * scale) * norm).astype(jnp.bfloat16)


def finish(scale, norm, kept, thin, col, chunk):
    seqs, cols = col.shape
    spots, args = [], []
    for terms, row, column, rows, width in kept:
        spots.append((len(terms), row, column, rows, width))
        args += terms
    return pl.pallas_call(
        functools.partial(finish_kernel, seqs, scale, norm, spots),
        out_shape=jax.ShapeDtypeStruct((chunk, cols), jnp.bfloat16),
        compiler_params=params(),
        cost_estimate=cost(12 * chunk * cols * seqs, 12 * chunk * cols),
    )(*args, thin, col)


def after(value, *others):
    return lax.optimization_barrier((value, *others))[0]


def shards(
    sizes,
    up_input,
    gate_pre,
    up_pre,
    grad_hidden,
    grad_output,
    proj_up_in,
    proj_up_out,
    proj_down_in,
    proj_down_out,
    gram,
    canaries,
):
    grp, dp, mp = sizes
    rank = proj_up_in.shape[0]
    seq_len = up_input.shape[1]
    rows_here, cols_here = gram.shape
    features = rows_here * grp * mp
    can_here, depth = canaries.shape
    chunk = can_here * dp // (grp * mp)
    seqs = grp * dp
    scale, norm = 1.0 / seqs, 1.0 / math.sqrt(features)
    me = lax.axis_index(("grp", "dp", "mp")).astype(jnp.int32).reshape(1)

    steps_grp = [("grp", grp, bit, bit * mp) for bit in bits_of(grp)]
    steps_mp = [("mp", mp, bit, bit) for bit in reversed(bits_of(mp))]
    grp_first, mp_first = steps_grp + steps_mp, steps_mp + steps_grp

    direct = can_here >= chunk
    half_rows = chunk // 2

    def spread_canaries(own, gate):
        blocks = {0: own}
        for bit in bits_of(dp):
            there = {at ^ bit: lax.ppermute(block, "dp", pairs(dp, bit)) for at, block in blocks.items()}
            blocks |= {at: after(block, gate) if bit > 1 else block for at, block in there.items()}
        return [blocks[at] for at in range(dp)]

    def begin(half, steps, start, width, gate):
        bits = [code for _, _, _, code in steps]
        (low,) = product(sizes, direct, bits, after(me, gate), halves[half], gram_low, [], start, width)
        return low

    def send(steps, low):
        axis, size, bit, _ = steps[0]
        return lax.ppermute(low, axis, pairs(size, bit))

    def add_first(half, steps, start, width, recv, gate):
        bits = [code for _, _, _, code in steps]
        low, keep = product(
            sizes, direct, bits, after(me, gate), halves[half], gram_low, [recv], start, width
        )
        axis, size, bit, _ = steps[1]
        return keep, [lax.ppermute(low, axis, pairs(size, bit))]

    def add_next(steps, keep, arrived, gate):
        left_over = 1 << (len(steps) - 1 - len(arrived))
        rows = (left_over // 2) * half_rows
        low = keep[:rows]
        for array in arrived:
            low = low + array[-left_over * half_rows :][:rows].astype(jnp.float32)
        low = after(low.astype(jnp.bfloat16), gate)
        axis, size, bit, _ = steps[len(arrived) + 1]
        return low, keep[rows:], [*arrived, lax.ppermute(low, axis, pairs(size, bit))]

    if direct:
        own = canaries.reshape(-1, 2, half_rows, depth)
    else:
        own = lax.all_gather(canaries, "dp", axis=0, tiled=True).reshape(-1, 2, half_rows, depth)

    order = [0]
    for _, _, _, code in reversed(steps_mp):
        order = [at | code for at in order] + order
    sent, token_sums, gram_here, gram_low = project_all(
        order, me, up_input, gate_pre, up_pre, grad_hidden, grad_output,
        proj_up_in, proj_up_out, proj_down_in, proj_down_out, gram,
    )
    halves = [spread_canaries(own[:, 0], gram_low) if direct else [own[:, 0]]]
    middle = cols_here // 2
    low_a = begin(0, grp_first, 0, middle, gram_low)
    recv_a = send(grp_first, low_a)
    gate = low_a
    for axis, size, bit, _ in steps_mp[:-1]:
        token_sums = token_sums[-sent.shape[0] :] + after(lax.ppermute(sent, axis, pairs(size, bit)), gate)
        sent = token_sums[: token_sums.shape[0] // 2]
    there = lax.ppermute(sent, "mp", pairs(mp, steps_mp[-1][2]))
    halves.append(spread_canaries(own[:, 1], token_sums) if direct else [own[:, 1]])
    low_c = begin(1, mp_first, middle, middle, token_sums)
    recv_c = send(mp_first, low_c)
    row = feature_rows(1.0 / math.sqrt(seq_len), rank, token_sums, after(there, low_c))[None]

    gathered = row
    low_d = begin(0, grp_first, middle, middle, row)
    recv_d = send(grp_first, low_d)
    keep_a, there_a = add_first(0, grp_first, 0, middle, recv_a, low_d)
    gate = keep_a
    for bit in bits_of(grp):
        gathered = jnp.concatenate([gathered, after(lax.ppermute(gathered, "grp", pairs(grp, bit)), gate)])
    low_b = begin(1, grp_first, 0, middle, gathered)
    gate = low_b
    for at, bit in enumerate(reversed(bits_of(mp))):
        gathered = gathered + after(lax.ppermute(gathered, "mp", pairs(mp, bit)), gate)
        if at == 0:
            keep_c, there_c = add_first(1, mp_first, middle, middle, recv_c, gathered)
            gate = keep_c
    recv_b = send(grp_first, after(low_b, gathered))
    keep_d, there_d = add_first(0, grp_first, middle, middle, recv_d, gathered)
    gate = keep_d
    for bit in bits_of(dp):
        gathered = jnp.concatenate([gathered, after(lax.ppermute(gathered, "dp", pairs(dp, bit)), gate)])
        if bit == bits_of(dp)[0]:
            low_a, keep_a, there_a = add_next(grp_first, keep_a, there_a, gathered)
            gate = low_a
    left, right, col = spread(me, gathered, dp, mp, rows_here, cols_here)
    thin = thin_products(
        sizes, direct, [code for _, _, _, code in grp_first], me, halves, gram_low, left, col
    )
    gram_new = update(scale, after(me, thin), gram_here, left, right)
    keep_b, there_b = add_first(1, grp_first, 0, middle, recv_b, gram_new)
    low_c, keep_c, there_c = add_next(mp_first, keep_c, there_c, keep_b)
    low_d, keep_d, there_d = add_next(grp_first, keep_d, there_d, low_c)
    gate = low_d
    for at, (axis, size, bit, _) in enumerate(grp_first):
        half = thin.shape[1] // 2
        thin = thin[:, half:] + after(lax.ppermute(thin[:, :half], axis, pairs(size, bit)), gate)
        if at == 0:
            low_b, keep_b, there_b = add_next(grp_first, keep_b, there_b, thin)
            gate = low_b
    scores = score(scale, norm * norm, thin, col)
    for bit in bits_of(dp):
        scores = scores + lax.ppermute(scores, "dp", pairs(dp, bit))
    kept = [
        ([keep_a, *there_a], 0, 0, half_rows, middle),
        ([keep_d, *there_d], 0, middle, half_rows, middle),
        ([keep_c, *there_c], half_rows, middle, half_rows, middle),
        ([keep_b, *there_b], half_rows, 0, half_rows, middle),
    ]
    mapped = finish(scale, norm, kept, thin, col, chunk)
    return gram_new, mapped, scores


def solution(mesh):
    sizes = tuple(mesh.shape[name] for name in ("grp", "dp", "mp"))
    wide = P(("grp", "dp"), None, "mp")
    return jax.shard_map(
        functools.partial(shards, sizes),
        mesh=mesh,
        in_specs=(wide, wide, wide, wide, wide)
        + (P(None, "mp"),) * 4
        + (P(("grp", "mp"), "dp"), P("dp", ("grp", "mp"))),
        out_specs=(P(("grp", "mp"), "dp"), P(("grp", "mp"), "dp"), P(None, ("grp", "mp"))),
        check_vma=False,
    )
```

```python
import functools
import math

import jax
import jax.numpy as jnp
from jax import lax
from jax.experimental import pallas as pl
from jax.experimental.pallas import tpu as pltpu
from jax.sharding import PartitionSpec as P

LANES = 128
NT = (((1,), (1,)), ((), ()))
TN = (((0,), (0,)), ((), ()))
VMEM_LIMIT = 24 * 1024 * 1024


def dot(a, b, dims, precision=None):
    return lax.dot_general(a, b, dims, precision=precision, preferred_element_type=jnp.float32)


def pairs(size, bit):
    return [(at, at ^ bit) for at in range(size)]


def bits_of(size):
    return [1 << at for at in reversed(range(size.bit_length() - 1))]


def params():
    return pltpu.CompilerParams(vmem_limit_bytes=VMEM_LIMIT)


def cost(flops, bytes_accessed):
    return pl.CostEstimate(flops=flops // 100, bytes_accessed=bytes_accessed // 100, transcendentals=0)


def project_kernel(order, tile, me, *refs):
    sources, (sent, kept, gram, gram_low), (held, whole, arrived) = refs[:10], refs[10:14], (refs[14:23], refs[23], refs[24])
    copies = {}

    def copy(name, source, target):
        one = pltpu.make_async_copy(source, target, arrived.at[len(copies)])
        one.start()
        copies[name] = one

    up_in, gate, up_pre, grad_h, grad_o, p_ui, p_uo, p_di, p_do, old = sources
    h_up_in, h_gate, h_up_pre, h_grad_h, h_grad_o, h_ui, h_uo, h_di, h_do = held
    starts = range(0, h_gate.shape[1], tile)
    for start in starts:
        part = pl.ds(start, tile)
        for name, source, target in (("gate", gate, h_gate), ("grad_h", grad_h, h_grad_h), ("up_pre", up_pre, h_up_pre)):
            copy((name, start), source.at[0, :, part], target.at[:, part])
        for name, source, target in (("uo", p_uo, h_uo), ("di", p_di, h_di)):
            copy((name, start), source.at[:, part], target.at[:, part])
    copy("up_in", up_in.at[0], h_up_in)
    copy("ui", p_ui, h_ui)
    copy("grad_o", grad_o.at[0], h_grad_o)
    copy("do", p_do, h_do)
    share = gram.shape[0] // 4
    for at in range(4):
        rows = pl.ds(at * share, share)
        copy(("gram", at), old.at[rows], gram.at[rows])

    out_up, in_down = 0.0, 0.0
    for start in starts:
        part = slice(start, start + tile)
        for name in ("gate", "grad_h", "up_pre", "uo", "di"):
            copies[name, start].wait()
        act = h_gate[:, part].astype(jnp.float32)
        act = act / (1.0 + jnp.exp(-act))
        grad_up = (h_grad_h[:, part].astype(jnp.float32) * act).astype(jnp.bfloat16)
        hidden = (act * h_up_pre[:, part].astype(jnp.float32)).astype(jnp.bfloat16)
        out_up = out_up + dot(grad_up, h_uo[:, part], NT)
        in_down = in_down + dot(hidden, h_di[:, part], NT)
    for name in ("up_in", "ui", "grad_o", "do"):
        copies[name].wait()
    in_up = dot(h_up_in[...], h_ui[...], NT)
    out_down = dot(h_grad_o[...], h_do[...], NT)
    whole[...] = jnp.concatenate([in_up, out_up, in_down, out_down], axis=1)
    rows = whole.shape[0] // len(order)
    own = me[0] % len(order)
    for at, code in enumerate(order):
        out = sent if at < len(order) // 2 else kept
        spot = at % (len(order) // 2) * rows
        out[spot : spot + rows, :] = whole[pl.ds(pl.multiple_of((own ^ code) * rows, rows), rows), :]
    for at in range(4):
        copies["gram", at].wait()
        rows = slice(at * share, (at + 1) * share)
        gram_low[rows, :] = gram[rows, :].astype(jnp.bfloat16)


def project_all(order, me, up_in, gate, up_pre, grad_h, grad_o, p_ui, p_uo, p_di, p_do, gram):
    _, seq, d_here = up_in.shape
    f_here = gate.shape[2]
    rank = p_ui.shape[0]
    tile = max(t for t in range(LANES, 897, LANES) if f_here % t == 0)
    arrays = (up_in, gate, up_pre, grad_h, grad_o, p_ui, p_uo, p_di, p_do)
    vmem = pl.BlockSpec(memory_space=pltpu.VMEM)
    return pl.pallas_call(
        functools.partial(project_kernel, order, tile),
        out_shape=[jax.ShapeDtypeStruct((seq // 2, 4 * rank), jnp.float32)] * 2
        + [jax.ShapeDtypeStruct(gram.shape, dtype) for dtype in (jnp.float32, jnp.bfloat16)],
        in_specs=[pl.BlockSpec(memory_space=pltpu.SMEM)] + [pl.BlockSpec(memory_space=pltpu.HBM)] * 10,
        out_specs=[vmem] * 4,
        scratch_shapes=[pltpu.VMEM(array.shape[-2:], array.dtype) for array in arrays]
        + [
            pltpu.VMEM((seq, 4 * rank), jnp.float32),
            pltpu.SemaphoreType.DMA((5 * (f_here // tile) + 8,)),
        ],
        compiler_params=params(),
        cost_estimate=cost(4 * seq * rank * (d_here + f_here), 6 * seq * f_here + 4 * seq * d_here),
    )(me, *(pltpu.with_memory_space_constraint(array, pltpu.HBM) for array in (*arrays, gram)))


def feature_kernel(norm, rank, mine, there, out, square):
    rows = there.shape[0]
    total = mine[mine.shape[0] - rows :, :] + there[...]
    half = rank * rank // LANES
    for at in range(2):
        left = total[:, (2 * at + 1) * rank : (2 * at + 2) * rank]
        right = total[:, 2 * at * rank : (2 * at + 1) * rank]
        square[...] = dot(left, right, TN, lax.Precision.HIGHEST) * norm
        step = LANES // rank
        out[at * half : (at + 1) * half, :] = jnp.concatenate(
            [square[pl.ds(lane, half, step), :] for lane in range(step)], axis=1
        )


def feature_rows(norm, rank, mine, there):
    return pl.pallas_call(
        functools.partial(feature_kernel, norm, rank),
        out_shape=jax.ShapeDtypeStruct((2 * rank * rank // LANES, LANES), jnp.float32),
        scratch_shapes=[pltpu.VMEM((rank, rank), jnp.float32)],
        compiler_params=params(),
        cost_estimate=cost(24 * rank * rank * there.shape[0], 100000),
    )(mine, there)


def spread_kernel(seqs, dp, mp, me, gathered, left, right, col, rows_f, cols_f):
    grp_at, dp_at, mp_at = me[0] // (dp * mp), (me[0] // mp) % dp, me[0] % mp
    own = grp_at * dp + dp_at
    row_at = grp_at * mp + mp_at
    count = seqs.bit_length() - 1
    row_groups, col_groups = rows_f.shape[1] // LANES, cols_f.shape[1] // LANES
    for seq in range(seqs):
        code = own ^ seq
        place = 0
        for bit in range(count):
            place = place + (((code >> bit) & 1) << (count - 1 - bit))
        for group in range(row_groups):
            rows_f[seq : seq + 1, group * LANES : (group + 1) * LANES] = gathered[
                place, pl.ds(row_at * row_groups + group, 1), :
            ]
        for group in range(col_groups):
            cols_f[seq : seq + 1, group * LANES : (group + 1) * LANES] = gathered[
                place, pl.ds(dp_at * col_groups + group, 1), :
            ]
    row, column = rows_f[...], cols_f[...]
    row_high = row.astype(jnp.bfloat16).astype(jnp.float32)
    col_high = column.astype(jnp.bfloat16).astype(jnp.float32)
    row_low, col_low = row - row_high, column - col_high
    for out, stack in (
        (left, [row_high, row_high, row_low]),
        (right, [col_high, col_low, col_high]),
    ):
        spare = out.shape[0] - len(stack) * seqs
        if spare:
            stack.append(jnp.zeros((spare, out.shape[1]), jnp.float32))
        out[...] = jnp.concatenate(stack).astype(jnp.bfloat16)
    col[...] = column


def spread(me, gathered, dp, mp, rows_here, cols_here):
    seqs = gathered.shape[0]
    deep = -(-3 * seqs // 16) * 16
    return pl.pallas_call(
        functools.partial(spread_kernel, seqs, dp, mp),
        out_shape=[
            jax.ShapeDtypeStruct((deep, rows_here), jnp.bfloat16),
            jax.ShapeDtypeStruct((deep, cols_here), jnp.bfloat16),
            jax.ShapeDtypeStruct((seqs, cols_here), jnp.float32),
        ],
        in_specs=[
            pl.BlockSpec(memory_space=pltpu.SMEM),
            pl.BlockSpec(memory_space=pltpu.VMEM),
        ],
        scratch_shapes=[
            pltpu.VMEM((seqs, rows_here), jnp.float32),
            pltpu.VMEM((seqs, cols_here), jnp.float32),
        ],
        compiler_params=params(),
        cost_estimate=cost(0, 1000000),
    )(me, gathered)


def update_kernel(scale, me, gram, left, right, out):
    rows = out.shape[0]
    at = pl.ds(pl.multiple_of(pl.program_id(0) * rows, rows), rows)
    out[...] = gram[at, :] + dot(left[...], right[...], TN) * scale


def update(scale, me, gram, left, right):
    rows, cols = gram.shape
    tile = min(rows, 512)
    deep = left.shape[0]
    return pl.pallas_call(
        functools.partial(update_kernel, scale),
        out_shape=jax.ShapeDtypeStruct(gram.shape, jnp.float32),
        grid=(rows // tile,),
        in_specs=[
            pl.BlockSpec(memory_space=pltpu.SMEM),
            pl.BlockSpec(memory_space=pltpu.VMEM),
            pl.BlockSpec((deep, tile), lambda i: (0, i)),
            pl.BlockSpec((deep, cols), lambda i: (0, 0)),
        ],
        out_specs=pl.BlockSpec((tile, cols), lambda i: (i, 0)),
        compiler_params=params(),
        cost_estimate=cost(2 * rows * cols * deep, 8 * rows * cols),
    )(me, gram, left, right)


def place(me, sizes, direct, bits, at, row, per):
    grp, dp, mp = sizes
    target = ((at ^ ((me // mp) % dp)) * per + row) if direct else row
    code = target ^ ((me // (dp * mp)) * mp + me % mp)
    spot = 0
    for bit in bits:
        spot = 2 * spot + (1 - ((code // bit) & 1))
    return spot


def sort_rows(me, sizes, direct, bits, first, count, cans, out):
    for at, can in enumerate(cans):
        for row in range(can.shape[0]):
            spot = place(me, sizes, direct, bits, at, row, can.shape[0]) - first

            @pl.when((spot >= 0) & (spot < count))
            def _(can=can, row=row, spot=spot):
                out[spot] = can[row]


def product_kernel(sizes, direct, bits, first, start, n_cans, n_recv, me, *refs):
    cans, gram, recvs, outs = refs[:n_cans], refs[n_cans], refs[n_cans + 1 : n_cans + 1 + n_recv], refs[n_cans + 1 + n_recv :]
    outs, rows = outs[:-1], outs[-1]
    low = outs[0]
    count, unit, depth = rows.shape
    sort_rows(me[0], sizes, direct, bits, first, count, cans, rows)
    width = low.shape[1]
    tile = next(tile for tile in (512, 256, 128) if width % tile == 0)
    for at in range(0, width, tile):
        value = dot(
            rows[...].reshape(count * unit, depth),
            gram[:, start + at : start + at + tile],
            (((1,), (0,)), ((), ())),
        )
        if not recvs:
            low[:, at : at + tile] = value.astype(jnp.bfloat16)
        else:
            value = value + recvs[0][:, at : at + tile].astype(jnp.float32)
            half = low.shape[0]
            low[:, at : at + tile] = value[:half].astype(jnp.bfloat16)
            outs[1][:, at : at + tile] = value[half:]


def product(sizes, direct, bits, me, cans, gram, recvs, start, width):
    depth = gram.shape[0]
    unit = cans[0].shape[1]
    count = sizes[0] * sizes[2] // 2
    rows = count * unit
    vmem = pl.BlockSpec(memory_space=pltpu.VMEM)
    args = [me, *cans, gram, *recvs]
    if recvs:
        out_shape = [
            jax.ShapeDtypeStruct((rows // 2, width), jnp.bfloat16),
            jax.ShapeDtypeStruct((rows // 2, width), jnp.float32),
        ]
    else:
        out_shape = [jax.ShapeDtypeStruct((rows, width), jnp.bfloat16)]
    first = count if recvs else 0
    return pl.pallas_call(
        functools.partial(product_kernel, sizes, direct, bits, first, start, len(cans), len(recvs)),
        out_shape=out_shape,
        in_specs=[pl.BlockSpec(memory_space=pltpu.SMEM)] + [vmem] * (len(args) - 1),
        out_specs=[vmem] * len(out_shape),
        scratch_shapes=[pltpu.VMEM((count, unit, depth), jnp.bfloat16)],
        compiler_params=params(),
        cost_estimate=cost(2 * rows * width * depth, 2 * depth * width + 2 * rows * (depth + width)),
    )(*args)


def thin_kernel(sizes, direct, bits, n_cans, seqs, me, *refs):
    halves = refs[:n_cans], refs[n_cans : 2 * n_cans]
    gram, row, col, out, rows = refs[2 * n_cans :]
    count, _, unit, depth = rows.shape
    for half, cans in enumerate(halves):
        for at, can in enumerate(cans):
            for spot in range(can.shape[0]):
                rows[place(me[0], sizes, direct, bits, at, spot, can.shape[0]), half] = can[spot]

    def stack(*values):
        split = []
        for value in values:
            high = value.astype(jnp.bfloat16).astype(jnp.float32)
            split += [high, value - high]
        spare = -len(split) * seqs % LANES
        if spare:
            split.append(jnp.zeros((spare, values[0].shape[1]), jnp.float32))
        return jnp.concatenate(split).astype(jnp.bfloat16)

    across = dot(gram[...], stack(col[...]), NT).T
    across = across[:seqs] + across[seqs : 2 * seqs]
    own = row[:seqs].astype(jnp.float32) + row[2 * seqs : 3 * seqs].astype(jnp.float32)
    value = dot(rows[...].reshape(-1, depth), stack(own, across), NT).T
    out[:seqs] = value[:seqs] + value[seqs : 2 * seqs]
    out[seqs:] = value[2 * seqs : 3 * seqs] + value[3 * seqs : 4 * seqs]


def thin_products(sizes, direct, bits, me, halves, gram, left, col):
    seqs = col.shape[0]
    count = sizes[0] * sizes[2]
    unit, depth = halves[0][0].shape[1:]
    rows = count * 2 * unit
    vmem = pl.BlockSpec(memory_space=pltpu.VMEM)
    args = [*halves[0], *halves[1], gram, left, col]
    return pl.pallas_call(
        functools.partial(thin_kernel, sizes, direct, bits, len(halves[0]), seqs),
        out_shape=jax.ShapeDtypeStruct((2 * seqs, rows), jnp.float32),
        in_specs=[pl.BlockSpec(memory_space=pltpu.SMEM)] + [vmem] * len(args),
        out_specs=vmem,
        scratch_shapes=[pltpu.VMEM((count, 2, unit, depth), jnp.bfloat16)],
        compiler_params=params(),
        cost_estimate=cost(256 * depth * (gram.shape[1] + rows), 2 * depth * (gram.shape[1] + rows)),
    )(me, *args)


def score_kernel(scale, norm, thin, col, out):
    column = col[...]
    seqs = column.shape[0]
    inner = dot(column, column, NT, lax.Precision.HIGHEST) * scale
    value = thin[seqs:] + dot(inner, thin[:seqs], (((1,), (0,)), ((), ())), lax.Precision.HIGHEST)
    out[...] = value * norm


def score(scale, norm, thin, col):
    return pl.pallas_call(
        functools.partial(score_kernel, scale, norm),
        out_shape=jax.ShapeDtypeStruct((col.shape[0], thin.shape[1]), jnp.float32),
        compiler_params=params(),
        cost_estimate=cost(12 * col.size * col.shape[0], 8 * col.size),
    )(thin, col)


def finish_kernel(seqs, scale, norm, spots, *refs):
    terms, (thin, col, mapped) = list(refs[:-3]), refs[-3:]
    for offsets, row, column, rows, width in spots:
        value = 0.0
        for offset in offsets:
            term = terms.pop(0)
            value = value + term[term.shape[0] - rows :, offset : offset + width].astype(jnp.float32)
        share = dot(thin[:seqs, row : row + rows], col[:, column : column + width], TN, lax.Precision.HIGHEST)
        mapped[row : row + rows, column : column + width] = ((value + share * scale) * norm).astype(jnp.bfloat16)


def finish(scale, norm, kept, thin, col, chunk):
    seqs, cols = col.shape
    spots, args = [], []
    for terms, row, column, rows, width in kept:
        spots.append(([offset for _, offset in terms], row, column, rows, width))
        args += [term for term, _ in terms]
    return pl.pallas_call(
        functools.partial(finish_kernel, seqs, scale, norm, spots),
        out_shape=jax.ShapeDtypeStruct((chunk, cols), jnp.bfloat16),
        compiler_params=params(),
        cost_estimate=cost(12 * chunk * cols * seqs, 12 * chunk * cols),
    )(*args, thin, col)


def after(value, *others):
    return lax.optimization_barrier((value, *others))[0]


def shards(
    sizes,
    up_input,
    gate_pre,
    up_pre,
    grad_hidden,
    grad_output,
    proj_up_in,
    proj_up_out,
    proj_down_in,
    proj_down_out,
    gram,
    canaries,
):
    grp, dp, mp = sizes
    rank = proj_up_in.shape[0]
    seq_len = up_input.shape[1]
    rows_here, cols_here = gram.shape
    features = rows_here * grp * mp
    can_here, depth = canaries.shape
    chunk = can_here * dp // (grp * mp)
    seqs = grp * dp
    scale, norm = 1.0 / seqs, 1.0 / math.sqrt(features)
    me = lax.axis_index(("grp", "dp", "mp")).astype(jnp.int32).reshape(1)

    steps_grp = [("grp", grp, bit, bit * mp) for bit in bits_of(grp)]
    steps_mp = [("mp", mp, bit, bit) for bit in reversed(bits_of(mp))]
    grp_first, mp_first = steps_grp + steps_mp, steps_mp + steps_grp

    direct = can_here >= chunk
    half_rows = chunk // 2

    def spread_canaries(own, gate):
        blocks = {0: own}
        for bit in bits_of(dp):
            there = {at ^ bit: lax.ppermute(block, "dp", pairs(dp, bit)) for at, block in blocks.items()}
            blocks |= {at: after(block, gate) if bit > 1 else block for at, block in there.items()}
        return [blocks[at] for at in range(dp)]

    def begin(half, steps, start, width, gate):
        bits = [code for _, _, _, code in steps]
        (low,) = product(sizes, direct, bits, after(me, gate), halves[half], gram_low, [], start, width)
        return low

    def send(steps, low):
        axis, size, bit, _ = steps[0]
        return lax.ppermute(low, axis, pairs(size, bit))

    def add_first(half, steps, start, width, recv, gate):
        bits = [code for _, _, _, code in steps]
        low, keep = product(
            sizes, direct, bits, after(me, gate), halves[half], gram_low, [recv], start, width
        )
        axis, size, bit, _ = steps[1]
        return keep, [lax.ppermute(low, axis, pairs(size, bit))]

    def add_next(steps, pieces, gate):
        left_over = 1 << (len(steps) - 1 - len(pieces[0][1]))
        rows = (left_over // 2) * half_rows
        lows, rest = [], []
        for keep, arrived in pieces:
            low = keep[:rows]
            for array in arrived:
                low = low + array[-left_over * half_rows :][:rows].astype(jnp.float32)
            lows.append(low.astype(jnp.bfloat16))
            rest.append((keep[rows:], arrived))
        low = after(jnp.concatenate(lows, axis=1) if lows[1:] else lows[0], gate)
        axis, size, bit, _ = steps[len(pieces[0][1]) + 1]
        return low, rest, lax.ppermute(low, axis, pairs(size, bit))

    if direct:
        own = canaries.reshape(-1, 2, half_rows, depth)
    else:
        own = lax.all_gather(canaries, "dp", axis=0, tiled=True).reshape(-1, 2, half_rows, depth)

    order = [0]
    for _, _, _, code in reversed(steps_mp):
        order = [at | code for at in order] + order
    sent, token_sums, gram_here, gram_low = project_all(
        order, me, up_input, gate_pre, up_pre, grad_hidden, grad_output,
        proj_up_in, proj_up_out, proj_down_in, proj_down_out, gram,
    )
    halves = [spread_canaries(own[:, 0], gram_low) if direct else [own[:, 0]]]
    middle = cols_here // 2
    split = cols_here // 2
    low_a = begin(0, grp_first, 0, middle, gram_low)
    recv_a = send(grp_first, low_a)
    low_d = begin(0, grp_first, middle, middle, low_a)
    gate = low_d
    for axis, size, bit, _ in steps_mp[:-1]:
        token_sums = token_sums[-sent.shape[0] :] + after(lax.ppermute(sent, axis, pairs(size, bit)), gate)
        sent = token_sums[: token_sums.shape[0] // 2]
    there = lax.ppermute(sent, "mp", pairs(mp, steps_mp[-1][2]))
    halves.append(spread_canaries(own[:, 1], token_sums) if direct else [own[:, 1]])
    low_c = begin(1, mp_first, split, cols_here - split, token_sums)
    recv_c = send(mp_first, low_c)
    row = feature_rows(1.0 / math.sqrt(seq_len), rank, token_sums, after(there, low_c))[None]

    gathered = row
    recv_d = send(grp_first, after(low_d, row))
    low_b = begin(1, grp_first, 0, split, row)
    keep_a, there_a = add_first(0, grp_first, 0, middle, recv_a, low_b)
    gate = keep_a
    for bit in bits_of(grp):
        gathered = jnp.concatenate([gathered, after(lax.ppermute(gathered, "grp", pairs(grp, bit)), gate)])
    for at, bit in enumerate(reversed(bits_of(mp))):
        gathered = gathered + after(lax.ppermute(gathered, "mp", pairs(mp, bit)), gate)
        if at == 0:
            recv_b = send(grp_first, after(low_b, gathered))
            keep_c, there_c = add_first(1, mp_first, split, cols_here - split, recv_c, gathered)
            gate = keep_c
    keep_d, there_d = add_first(0, grp_first, middle, middle, recv_d, gathered)
    gate = keep_d
    for bit in bits_of(dp):
        gathered = jnp.concatenate([gathered, after(lax.ppermute(gathered, "dp", pairs(dp, bit)), gate)])
    left, right, col = spread(me, gathered, dp, mp, rows_here, cols_here)
    thin = thin_products(
        sizes, direct, [code for _, _, _, code in grp_first], me, halves, gram_low, left, col
    )
    low_a, ((keep_a, there_a), (keep_d, there_d)), last_a = add_next(
        grp_first, [(keep_a, there_a), (keep_d, there_d)], thin
    )
    keep_b, there_b = add_first(1, grp_first, 0, split, recv_b, low_a)
    gate = keep_b
    for at, (axis, size, bit, _) in enumerate(grp_first):
        half = thin.shape[1] // 2
        thin = thin[:, half:] + after(lax.ppermute(thin[:, :half], axis, pairs(size, bit)), gate)
        if at == 0:
            gram_new = update(scale, after(me, thin), gram_here, left, right)
            low_c, ((keep_c, there_c),), last_c = add_next(mp_first, [(keep_c, there_c)], gram_new)
            low_b, ((keep_b, there_b),), last_b = add_next(grp_first, [(keep_b, there_b)], low_c)
            gate = low_b
        elif at == 1:
            last_a = after(last_a, after(low_b, thin)).astype(jnp.float32)
            sum_a = [
                keep + there[0][-half_rows:].astype(jnp.float32) + last_a[:, at : at + middle]
                for keep, there, at in ((keep_a, there_a, 0), (keep_d, there_d, middle))
            ]
            gate = sum_a[0]
    scores = score(scale, norm * norm, thin, col)
    whole = lambda keep, arrived, last: [(keep, 0), *((array, 0) for array in arrived), (last, 0)]
    kept = [
        ([(sum_a[0], 0)], 0, 0, half_rows, middle),
        ([(sum_a[1], 0)], 0, middle, half_rows, middle),
        (whole(keep_c, there_c, last_c), half_rows, split, half_rows, cols_here - split),
        (whole(keep_b, there_b, last_b), half_rows, 0, half_rows, split),
    ]
    mapped = finish(scale, norm, kept, thin, col, chunk)
    gate = mapped
    for bit in bits_of(dp):
        scores = scores + after(lax.ppermute(scores, "dp", pairs(dp, bit)), gate)
    return gram_new, mapped, scores


def solution(mesh):
    sizes = tuple(mesh.shape[name] for name in ("grp", "dp", "mp"))
    wide = P(("grp", "dp"), None, "mp")
    return jax.shard_map(
        functools.partial(shards, sizes),
        mesh=mesh,
        in_specs=(wide, wide, wide, wide, wide)
        + (P(None, "mp"),) * 4
        + (P(("grp", "mp"), "dp"), P("dp", ("grp", "mp"))),
        out_specs=(P(("grp", "mp"), "dp"), P(("grp", "mp"), "dp"), P(None, ("grp", "mp"))),
        check_vma=False,
    )
```
